512 devices in a mesh: grp: 8 (over y), wide: 64 (over x, z, core).
Axes of the slice: x: 4, y: 8, z: 8, core: 2. Of those that a mesh axis runs over, the one named last changes fastest.
Arguments:
- subspace: float32 [16384, 2048], P('wide', 'grp'), may hold values from -6 to 6
- hblocks: float32 [256, 16, 64, 64], P('wide'), may hold values from -0.1875 to 0.1875
- pattern: int32 [256, 16], P('wide'), may hold values from 0 to 255, as said below
- rotation: float32 [2048, 2048], P('grp'), may hold values from -0.125 to 0.125
Outputs:
- rotated: float32 [16384, 2048], P('wide', 'grp')
- correlation: float32 [2048, 256], P(('grp', 'wide'))
The draws below stay inside these ranges and needn't reach their ends.
Inputs may be any that keep to these rules, and one draw needn't show every extreme that they name: `pattern`: slot 0 of row block i is i itself. Every named block lies on an index of wide (counting around the axis as a loop) at most 2 from that of its row block, atom blocks with the same value of i // 4 lying on one index of wide; each row block has slots at distance 2 on both sides. Blocks may repeat within a row.
All inputs are finite; a program needn't handle non-finite values.
Results may differ from the reference program's by a relative error of at most 0.0001.
Values sent between devices are 32-bit elements; how exact they have to be, the bound alone decides.
No kernel may reach another device: no remote copies, remote signals or barrier semaphores. Data moves between devices by JAX's collectives and lax.ppermute only.
A program may use at most 64 MiB of HBM per device.

```python
import jax
import jax.numpy as jnp
from jax import lax

B = 64
M = 2048
A_DEV = 4
NB = 16
HW = 2
DEGREE = 4
NBLK = 256
NROWS = 16384
N_GRP = 8


def draw_pattern(key, part):
    devcount = NBLK // A_DEV
    rowids = jnp.arange(NBLK, dtype=jnp.int32)
    homes = rowids // A_DEV
    first, second = jax.random.split(jax.random.fold_in(key, 7))
    offsets = jax.random.randint(first, (NBLK, NB), -HW, HW + 1, dtype=jnp.int32)
    locals_drawn = jax.random.randint(second, (NBLK, NB), 0, A_DEV, dtype=jnp.int32)
    column = jnp.arange(NB, dtype=jnp.int32)[None, :]
    offsets = jnp.where(column == 0, 0, offsets)
    offsets = jnp.where(column == 1, HW, offsets)
    offsets = jnp.where(column == 2, -HW, offsets)
    locals_drawn = jnp.where(column == 0, (rowids % A_DEV)[:, None], locals_drawn)
    locals_drawn = jnp.where(column == 1, A_DEV - 1, locals_drawn)
    locals_drawn = jnp.where(column == 2, 0, locals_drawn)
    target = (homes[:, None] + offsets + devcount) % devcount
    return (target * A_DEV + locals_drawn).astype(jnp.int32)


def block_levels(rng, shape, cuts, least, high):
    gain = 1.0
    for dim, shards_of in cuts:
        steps = jax.random.uniform(jax.random.fold_in(jax.random.fold_in(rng, 6), dim), (shards_of,), jnp.float32, least / len(cuts), high / len(cuts))
        gain = gain * jnp.repeat(jnp.exp(steps), shape[dim] // shards_of).reshape((-1,) + (1,) * (len(shape) - 1 - dim))
    return gain


def centred(rng, dims, spread, bound, shards=(), kind=jnp.bfloat16):
    result = spread * jax.random.normal(rng, dims, jnp.float32)
    if shards:
        result = result * block_levels(rng, dims, shards, -0.22, 0.18)
    return jnp.clip(result, -bound, bound).astype(kind)


def setup_inputs(seed: int = 0) -> dict:
    key_of = jax.random.split(jax.random.key(seed), 5)
    subspace = centred(key_of[0], (NROWS, M), 1.0, 6.0, ((0, 64), (1, 8)), jnp.float32)
    hblocks = centred(key_of[1], (NBLK, NB, B, B), (NB * B) ** -0.5, 0.1875, ((0, 64),), jnp.float32)
    pattern = draw_pattern(jax.random.fold_in(key_of[4], 71), 0)
    rotation = centred(key_of[3], (M, M), M ** -0.5, 0.125, ((0, 8),), jnp.float32)
    return dict(subspace=subspace, hblocks=hblocks, pattern=pattern, rotation=rotation)


cheb_center = 0.25
cheb_half = 2.0


def apply_ham(field, hblocks, pattern):
    blocks = field.reshape(NBLK, B, M)

    def slot_term(total, items):
        hslot, column = items
        picked = jnp.take(blocks, column, axis=0)
        term = jnp.einsum("aij,ajc->aic", hslot, picked, precision=lax.Precision.HIGHEST)
        return total + term, None

    start = jnp.zeros((NBLK, B, M), jnp.float32)
    total, unused = lax.scan(slot_term, start, (jnp.transpose(hblocks, (1, 0, 2, 3)), jnp.transpose(pattern)))
    return total.reshape(NROWS, M)


def reference(subspace, hblocks, pattern, rotation):
    previous = subspace
    current = (apply_ham(subspace, hblocks, pattern) - cheb_center * subspace) / cheb_half
    for step in range(DEGREE - 1):
        nextone = 2.0 * (apply_ham(current, hblocks, pattern) - cheb_center * current) / cheb_half - previous
        previous = current
        current = nextone
    filtered = current
    grouped = filtered.reshape(NROWS, N_GRP, M // N_GRP)
    correlation = jnp.einsum("rgc,rgk->gck", grouped, grouped, precision=lax.Precision.HIGHEST) / NROWS
    correlation = correlation.reshape(M, M // N_GRP)
    rotated = jnp.dot(filtered, rotation, precision=lax.Precision.HIGHEST, preferred_element_type=jnp.float32)
    return rotated, correlation
```

```python
import jax
import jax.numpy as jnp
from jax import lax
from jax.sharding import PartitionSpec as P

B = 64
A_DEV = 4
NB = 16
HW = 2
DEGREE = 4


cheb_center = 0.25
cheb_half = 2.0

HI = lax.Precision.HIGHEST


def passed_along(value, axis, steps):
    count = lax.axis_size(axis)
    pairs = [(source, (source + steps) % count) for source in range(count)]
    return lax.ppermute(value, axis, pairs)


def dense_hamiltonian(hblocks, slot_index):
    local_blocks = hblocks.shape[0]
    window_blocks = (2 * HW + 1) * A_DEV
    onehot = (slot_index[:, :, None] == jnp.arange(window_blocks)[None, None, :]).astype(jnp.float32)
    hd = jnp.einsum("asp,asij->aipj", onehot, hblocks, precision=HI)
    return hd.reshape(local_blocks * B, window_blocks * B)


def apply_ham(field, hdense):
    rows = field.shape[0]
    pieces = [
        passed_along(field, "wide", 2),
        passed_along(field, "wide", 1),
        field,
        passed_along(field, "wide", -1),
        passed_along(field, "wide", -2),
    ]
    total = None
    for idx in (2, 1, 3, 0, 4):
        term = jnp.dot(hdense[:, idx * rows:(idx + 1) * rows], pieces[idx], precision=HI,
                       preferred_element_type=jnp.float32)
        total = term if total is None else total + term
    return total


def butterfly_scatter(value, axis):
    count = lax.axis_size(axis)
    me = lax.axis_index(axis)
    piece = value.shape[0] // count
    buf = value.reshape((count, piece) + value.shape[1:])
    bit = 0
    while (1 << bit) < count:
        n = buf.shape[0]
        buf = buf.reshape((n // 2, 2) + buf.shape[1:])
        mine = (me >> bit) & 1
        keep = jnp.where(mine == 0, buf[:, 0], buf[:, 1])
        send = jnp.where(mine == 0, buf[:, 1], buf[:, 0])
        pairs = [(i, i ^ (1 << bit)) for i in range(count)]
        buf = keep + lax.ppermute(send, axis, pairs)
        bit += 1
    return buf.reshape((piece,) + value.shape[1:])


def local(subspace, hblocks, pattern, rotation):
    devcount = lax.axis_size("wide")
    myself = lax.axis_index("wide")
    owner = pattern // A_DEV
    relative = (owner - myself + HW + devcount) % devcount
    slot_index = relative * A_DEV + pattern % A_DEV
    hdense = dense_hamiltonian(hblocks, slot_index)
    previous = subspace
    current = (apply_ham(subspace, hdense) - cheb_center * subspace) / cheb_half
    for step in range(DEGREE - 1):
        nextone = (
            2.0 * (apply_ham(current, hdense) - cheb_center * current) / cheb_half
            - previous
        )
        previous = current
        current = nextone
    total_rows = current.shape[0] * devcount
    gram_term = lax.dot_general(
        current,
        current,
        (((0,), (0,)), ((), ())),
        precision=HI,
        preferred_element_type=jnp.float32,
    )
    correlation = butterfly_scatter(gram_term, "wide") / total_rows
    rot_term = jnp.dot(
        current, rotation, precision=HI, preferred_element_type=jnp.float32
    )
    rotated = lax.psum_scatter(rot_term, "grp", scatter_dimension=1, tiled=True)
    return (rotated, correlation)


def solution(mesh):
    in_specs = (P("wide", "grp"), P("wide", None, None, None), P("wide", None), P("grp", None))
    out_specs = (P("wide", "grp"), P(("grp", "wide"), None))
    return jax.shard_map(local, mesh=mesh, in_specs=in_specs, out_specs=out_specs, check_vma=False)
```

```python
import jax
import jax.numpy as jnp
from jax import lax
from jax.sharding import PartitionSpec as P

B = 64
A_DEV = 4
NB = 16
HW = 2
DEGREE = 4


cheb_center = 0.25
cheb_half = 2.0

HI = lax.Precision.HIGHEST


def passed_along(value, axis, steps):
    count = lax.axis_size(axis)
    pairs = [(source, (source + steps) % count) for source in range(count)]
    return lax.ppermute(value, axis, pairs)


def dense_hamiltonian(hblocks, slot_index):
    local_blocks = hblocks.shape[0]
    window_blocks = (2 * HW + 1) * A_DEV
    onehot = (slot_index[:, :, None] == jnp.arange(window_blocks)[None, None, :]).astype(jnp.float32)
    hd = jnp.einsum("asp,asij->aipj", onehot, hblocks, precision=HI)
    return hd.reshape(local_blocks * B, window_blocks * B)


def apply_ham(field, hdense):
    rows = field.shape[0]
    pieces = [
        passed_along(field, "wide", 2),
        passed_along(field, "wide", 1),
        field,
        passed_along(field, "wide", -1),
        passed_along(field, "wide", -2),
    ]
    total = None
    for idx in (2, 1, 3, 0, 4):
        term = jnp.dot(hdense[:, idx * rows:(idx + 1) * rows], pieces[idx], precision=HI,
                       preferred_element_type=jnp.float32)
        total = term if total is None else total + term
    return total


def butterfly_scatter(value, axis):
    count = lax.axis_size(axis)
    me = lax.axis_index(axis)
    piece = value.shape[0] // count
    buf = value.reshape((count, piece) + value.shape[1:])
    bit = 0
    while (1 << bit) < count:
        n = buf.shape[0]
        buf = buf.reshape((n // 2, 2) + buf.shape[1:])
        mine = (me >> bit) & 1
        keep = jnp.where(mine == 0, buf[:, 0], buf[:, 1])
        send = jnp.where(mine == 0, buf[:, 1], buf[:, 0])
        pairs = [(i, i ^ (1 << bit)) for i in range(count)]
        buf = keep + lax.ppermute(send, axis, pairs)
        bit += 1
    return buf.reshape((piece,) + value.shape[1:])


def local(subspace, hblocks, pattern, rotation):
    devcount = lax.axis_size("wide")
    myself = lax.axis_index("wide")
    owner = pattern // A_DEV
    relative = (owner - myself + HW + devcount) % devcount
    slot_index = relative * A_DEV + pattern % A_DEV
    hdense = dense_hamiltonian(hblocks, slot_index)
    previous = subspace
    current = (apply_ham(subspace, hdense) - cheb_center * subspace) / cheb_half
    for step in range(DEGREE - 1):
        nextone = (
            2.0 * (apply_ham(current, hdense) - cheb_center * current) / cheb_half
            - previous
        )
        previous = current
        current = nextone
    total_rows = current.shape[0] * devcount
    gram_term = lax.dot_general(
        current,
        current,
        (((0,), (0,)), ((), ())),
        precision=HI,
        preferred_element_type=jnp.float32,
    )
    pieces = gram_term.reshape(devcount, -1, gram_term.shape[1])
    gathered = lax.all_to_all(pieces, "wide", 0, 0, tiled=True)
    correlation = jnp.sum(gathered, axis=0) / total_rows
    rot_term = jnp.dot(
        current, rotation, precision=HI, preferred_element_type=jnp.float32
    )
    half = rot_term.shape[0] // 2
    rotated = jnp.concatenate(
        [
            lax.psum_scatter(rot_term[:half], "grp", scatter_dimension=1, tiled=True),
            lax.psum_scatter(rot_term[half:], "grp", scatter_dimension=1, tiled=True),
        ],
        axis=0,
    )
    return (rotated, correlation)


def solution(mesh):
    in_specs = (P("wide", "grp"), P("wide", None, None, None), P("wide", None), P("grp", None))
    out_specs = (P("wide", "grp"), P(("grp", "wide"), None))
    return jax.shard_map(local, mesh=mesh, in_specs=in_specs, out_specs=out_specs, check_vma=False)
```

```python
import jax
import jax.numpy as jnp
from jax import lax
from jax.sharding import PartitionSpec as P

B = 64
A_DEV = 4
NB = 16
HW = 2
DEGREE = 4


cheb_center = 0.25
cheb_half = 2.0

HI = lax.Precision.HIGHEST


def passed_along(value, axis, steps):
    count = lax.axis_size(axis)
    pairs = [(source, (source + steps) % count) for source in range(count)]
    return lax.ppermute(value, axis, pairs)


def dense_hamiltonian(hblocks, slot_index):
    local_blocks = hblocks.shape[0]
    window_blocks = (2 * HW + 1) * A_DEV
    onehot = (slot_index[:, :, None] == jnp.arange(window_blocks)[None, None, :]).astype(jnp.float32)
    hd = jnp.einsum("asp,asij->aipj", onehot, hblocks, precision=HI)
    return hd.reshape(local_blocks * B, window_blocks * B)


def apply_ham(field, hdense):
    rows = field.shape[0]
    pieces = [
        passed_along(field, "wide", 2),
        passed_along(field, "wide", 1),
        field,
        passed_along(field, "wide", -1),
        passed_along(field, "wide", -2),
    ]
    total = None
    for idx in (2, 1, 3, 0, 4):
        term = jnp.dot(hdense[:, idx * rows:(idx + 1) * rows], pieces[idx], precision=HI,
                       preferred_element_type=jnp.float32)
        total = term if total is None else total + term
    return total


def butterfly_scatter(value, axis):
    count = lax.axis_size(axis)
    me = lax.axis_index(axis)
    piece = value.shape[0] // count
    buf = value.reshape((count, piece) + value.shape[1:])
    bit = 0
    while (1 << bit) < count:
        n = buf.shape[0]
        buf = buf.reshape((n // 2, 2) + buf.shape[1:])
        mine = (me >> bit) & 1
        keep = jnp.where(mine == 0, buf[:, 0], buf[:, 1])
        send = jnp.where(mine == 0, buf[:, 1], buf[:, 0])
        pairs = [(i, i ^ (1 << bit)) for i in range(count)]
        buf = keep + lax.ppermute(send, axis, pairs)
        bit += 1
    return buf.reshape((piece,) + value.shape[1:])


def local(subspace, hblocks, pattern, rotation):
    devcount = lax.axis_size("wide")
    myself = lax.axis_index("wide")
    owner = pattern // A_DEV
    relative = (owner - myself + HW + devcount) % devcount
    slot_index = relative * A_DEV + pattern % A_DEV
    hdense = dense_hamiltonian(hblocks, slot_index)
    previous = subspace
    current = (apply_ham(subspace, hdense) - cheb_center * subspace) / cheb_half
    for step in range(DEGREE - 1):
        nextone = (
            2.0 * (apply_ham(current, hdense) - cheb_center * current) / cheb_half
            - previous
        )
        previous = current
        current = nextone
    total_rows = current.shape[0] * devcount
    gram_term = lax.dot_general(
        current,
        current,
        (((0,), (0,)), ((), ())),
        precision=HI,
        preferred_element_type=jnp.float32,
    )
    pieces = gram_term.reshape(devcount, -1, gram_term.shape[1])
    gathered = lax.all_to_all(pieces, "wide", 0, 0, tiled=True)
    correlation = jnp.sum(gathered, axis=0) / total_rows
    ngrp = lax.axis_size("grp")
    width = current.shape[1]
    rot_blocks = jnp.einsum(
        "rk,kgn->grn", current, rotation.reshape(rotation.shape[0], ngrp, width),
        precision=HI, preferred_element_type=jnp.float32,
    )
    rot_parts = lax.all_to_all(rot_blocks, "grp", 0, 0, tiled=True)
    rotated = jnp.sum(rot_parts, axis=0)
    return (rotated, correlation)


def solution(mesh):
    in_specs = (P("wide", "grp"), P("wide", None, None, None), P("wide", None), P("grp", None))
    out_specs = (P("wide", "grp"), P(("grp", "wide"), None))
    return jax.shard_map(local, mesh=mesh, in_specs=in_specs, out_specs=out_specs, check_vma=False)
```

```python
import jax
import jax.numpy as jnp
from jax import lax
from jax.sharding import PartitionSpec as P

B = 64
A_DEV = 4
NB = 16
HW = 2
DEGREE = 4


cheb_center = 0.25
cheb_half = 2.0

HI = lax.Precision.HIGHEST


def mm(a, b):
    return jnp.dot(a, b, precision=HI, preferred_element_type=jnp.float32)


def dense_hamiltonian(hblocks, slot_index):
    local_blocks = hblocks.shape[0]
    window_blocks = (2 * HW + 1) * A_DEV
    onehot = (slot_index[:, :, None] == jnp.arange(window_blocks)[None, None, :]).astype(jnp.float32)
    hd = jnp.einsum("asp,asij->aipj", onehot, hblocks, precision=HI)
    return hd.reshape(local_blocks * B, window_blocks * B)


def local(subspace, hblocks, pattern, rotation):
    devcount = lax.axis_size("wide")
    myself = lax.axis_index("wide")
    chips = devcount // 2
    core = myself % 2
    rows = subspace.shape[0]

    swap_pairs = [(i, i ^ 1) for i in range(devcount)]
    near_pairs = []
    for q in range(chips):
        near_pairs.append((2 * ((q - 1) % chips), 2 * q))
        near_pairs.append((2 * ((q + 1) % chips) + 1, 2 * q + 1))

    owner = pattern // A_DEV
    relative = (owner - myself + HW + devcount) % devcount
    slot_index = relative * A_DEV + pattern % A_DEV
    hd_own = dense_hamiltonian(hblocks, slot_index)
    zeros = jnp.zeros((rows, rows), jnp.float32)
    hc_own = jnp.where(core == 0,
                       jnp.concatenate([hd_own, zeros], axis=1),
                       jnp.concatenate([zeros, hd_own], axis=1))
    hc_other = lax.ppermute(hc_own, "wide", swap_pairs)
    sub_other = lax.ppermute(subspace, "wide", swap_pairs)
    first = core == 0
    h_chip = jnp.where(first, jnp.concatenate([hc_own, hc_other], axis=0),
                       jnp.concatenate([hc_other, hc_own], axis=0))
    y0 = jnp.where(first, jnp.concatenate([subspace, sub_other], axis=0),
                   jnp.concatenate([sub_other, subspace], axis=0))
    h_lo = h_chip[:, 0:2 * rows]
    h_self = h_chip[:, 2 * rows:4 * rows]
    h_hi = h_chip[:, 4 * rows:6 * rows]
    h_r1 = jnp.where(first, h_lo, h_hi)
    h_r2 = jnp.where(first, h_hi, h_lo)

    def apply_ham(field):
        r1 = lax.ppermute(field, "wide", near_pairs)
        total, r1 = lax.optimization_barrier((mm(h_self, field), r1))
        r2 = lax.ppermute(r1, "wide", swap_pairs)
        total, r2 = lax.optimization_barrier((total + mm(h_r1, r1), r2))
        return total + mm(h_r2, r2)

    previous = y0
    current = (apply_ham(y0) - cheb_center * y0) / cheb_half
    def cheb_step(step, carry):
        previous, current = carry
        nextone = (
            2.0 * (apply_ham(current) - cheb_center * current) / cheb_half
            - previous
        )
        return (current, nextone)

    previous, current = lax.fori_loop(0, DEGREE - 1, cheb_step, (previous, current))
    mine = lax.dynamic_slice_in_dim(current, core * rows, rows, axis=0)
    total_rows = rows * devcount
    gram_term = lax.dot_general(
        mine, mine, (((0,), (0,)), ((), ())), precision=HI, preferred_element_type=jnp.float32
    )
    pieces = gram_term.reshape(devcount, -1, gram_term.shape[1])
    gathered = lax.all_to_all(pieces, "wide", 0, 0, tiled=True)
    correlation = jnp.sum(gathered, axis=0) / total_rows
    rot_term = mm(mine, rotation)
    rotated = lax.psum_scatter(rot_term, "grp", scatter_dimension=1, tiled=True)
    return (rotated, correlation)


def solution(mesh):
    in_specs = (P("wide", "grp"), P("wide", None, None, None), P("wide", None), P("grp", None))
    out_specs = (P("wide", "grp"), P(("grp", "wide"), None))
    return jax.shard_map(local, mesh=mesh, in_specs=in_specs, out_specs=out_specs, check_vma=False)
```

```python
import jax
import jax.numpy as jnp
from jax import lax
from jax.sharding import PartitionSpec as P

B = 64
A_DEV = 4
NB = 16
HW = 2
DEGREE = 4


cheb_center = 0.25
cheb_half = 2.0

HI = lax.Precision.HIGHEST


def passed_along(value, axis, steps):
    count = lax.axis_size(axis)
    pairs = [(source, (source + steps) % count) for source in range(count)]
    return lax.ppermute(value, axis, pairs)


def dense_hamiltonian(hblocks, slot_index):
    local_blocks = hblocks.shape[0]
    window_blocks = (2 * HW + 1) * A_DEV
    hits = slot_index[:, :, None] == jnp.arange(window_blocks)[None, None, :]
    hd = jnp.sum(jnp.where(hits[:, :, None, :, None], hblocks[:, :, :, None, :], 0.0), axis=1)
    return hd.reshape(local_blocks * B, window_blocks * B)


def apply_ham(field, hdense):
    rows = field.shape[0]
    pieces = [
        passed_along(field, "wide", 2),
        passed_along(field, "wide", 1),
        field,
        passed_along(field, "wide", -1),
        passed_along(field, "wide", -2),
    ]
    total = None
    for idx in (2, 1, 3, 0, 4):
        term = jnp.dot(hdense[:, idx * rows:(idx + 1) * rows], pieces[idx], precision=HI,
                       preferred_element_type=jnp.float32)
        total = term if total is None else total + term
    return total


def butterfly_scatter(value, axis):
    count = lax.axis_size(axis)
    me = lax.axis_index(axis)
    piece = value.shape[0] // count
    buf = value.reshape((count, piece) + value.shape[1:])
    bit = 0
    while (1 << bit) < count:
        n = buf.shape[0]
        buf = buf.reshape((n // 2, 2) + buf.shape[1:])
        mine = (me >> bit) & 1
        keep = jnp.where(mine == 0, buf[:, 0], buf[:, 1])
        send = jnp.where(mine == 0, buf[:, 1], buf[:, 0])
        pairs = [(i, i ^ (1 << bit)) for i in range(count)]
        buf = keep + lax.ppermute(send, axis, pairs)
        bit += 1
    return buf.reshape((piece,) + value.shape[1:])


def local(subspace, hblocks, pattern, rotation):
    devcount = lax.axis_size("wide")
    myself = lax.axis_index("wide")
    owner = pattern // A_DEV
    relative = (owner - myself + HW + devcount) % devcount
    slot_index = relative * A_DEV + pattern % A_DEV
    hdense = dense_hamiltonian(hblocks, slot_index)
    previous = subspace
    current = (apply_ham(subspace, hdense) - cheb_center * subspace) / cheb_half
    def cheb_step(step, carry):
        previous, current = carry
        nextone = (
            2.0 * (apply_ham(current, hdense) - cheb_center * current) / cheb_half
            - previous
        )
        return (current, nextone)

    previous, current = lax.fori_loop(0, DEGREE - 1, cheb_step, (previous, current))
    total_rows = current.shape[0] * devcount
    gram_term = lax.dot_general(
        current,
        current,
        (((0,), (0,)), ((), ())),
        precision=HI,
        preferred_element_type=jnp.float32,
    )
    pieces = gram_term.reshape(devcount, -1, gram_term.shape[1])
    gathered = lax.all_to_all(pieces, "wide", 0, 0, tiled=True)
    correlation = jnp.sum(gathered, axis=0) / total_rows
    rot_term = jnp.dot(
        current, rotation, precision=HI, preferred_element_type=jnp.float32
    )
    rotated = lax.psum_scatter(rot_term, "grp", scatter_dimension=1, tiled=True)
    return (rotated, correlation)


def solution(mesh):
    in_specs = (P("wide", "grp"), P("wide", None, None, None), P("wide", None), P("grp", None))
    out_specs = (P("wide", "grp"), P(("grp", "wide"), None))
    return jax.shard_map(local, mesh=mesh, in_specs=in_specs, out_specs=out_specs, check_vma=False)
```

```python
import jax
import jax.numpy as jnp
from jax import lax
from jax.sharding import PartitionSpec as P

B = 64
A_DEV = 4
NB = 16
HW = 2
DEGREE = 4


cheb_center = 0.25
cheb_half = 2.0

HI = lax.Precision.HIGHEST


def passed_along(value, axis, steps):
    count = lax.axis_size(axis)
    pairs = [(source, (source + steps) % count) for source in range(count)]
    return lax.ppermute(value, axis, pairs)


def dense_hamiltonian(hblocks, slot_index):
    local_blocks = hblocks.shape[0]
    window_blocks = (2 * HW + 1) * A_DEV
    onehot = (slot_index[:, :, None] == jnp.arange(window_blocks)[None, None, :]).astype(jnp.float32)
    hd = jnp.einsum("asp,asij->aipj", onehot, hblocks, precision=HI)
    return hd.reshape(local_blocks * B, window_blocks * B)


def apply_ham(field, hdense):
    rows = field.shape[0]
    pieces = [
        passed_along(field, "wide", 2),
        passed_along(field, "wide", 1),
        field,
        passed_along(field, "wide", -1),
        passed_along(field, "wide", -2),
    ]
    total = None
    for idx in (2, 1, 3, 0, 4):
        term = jnp.dot(hdense[:, idx * rows:(idx + 1) * rows], pieces[idx], precision=HI,
                       preferred_element_type=jnp.float32)
        total = term if total is None else total + term
    return total


def local(subspace, hblocks, pattern, rotation):
    devcount = lax.axis_size("wide")
    myself = lax.axis_index("wide")
    owner = pattern // A_DEV
    relative = (owner - myself + HW + devcount) % devcount
    slot_index = relative * A_DEV + pattern % A_DEV
    hdense = dense_hamiltonian(hblocks, slot_index)
    previous = subspace
    current = (apply_ham(subspace, hdense) - cheb_center * subspace) / cheb_half
    for step in range(DEGREE - 1):
        nextone = (
            2.0 * (apply_ham(current, hdense) - cheb_center * current) / cheb_half
            - previous
        )
        previous = current
        current = nextone
    total_rows = current.shape[0] * devcount
    gram_term = lax.dot_general(
        current,
        current,
        (((0,), (0,)), ((), ())),
        precision=HI,
        preferred_element_type=jnp.float32,
    )
    pieces = gram_term.reshape(devcount, -1, gram_term.shape[1])
    gathered = lax.all_to_all(pieces, "wide", 0, 0, tiled=True)
    correlation = jnp.sum(gathered, axis=0) / total_rows
    rot_term = jnp.dot(
        current, rotation, precision=HI, preferred_element_type=jnp.float32
    )
    rotated = lax.psum_scatter(rot_term, "grp", scatter_dimension=1, tiled=True)
    return (rotated, correlation)


def solution(mesh):
    in_specs = (P("wide", "grp"), P("wide", None, None, None), P("wide", None), P("grp", None))
    out_specs = (P("wide", "grp"), P(("grp", "wide"), None))
    return jax.shard_map(local, mesh=mesh, in_specs=in_specs, out_specs=out_specs, check_vma=False)
```

```python
import jax
import jax.numpy as jnp
from jax import lax
from jax.sharding import PartitionSpec as P

B = 64
A_DEV = 4
NB = 16
HW = 2
DEGREE = 4


cheb_center = 0.25
cheb_half = 2.0

HI = lax.Precision.HIGHEST


def dense_hamiltonian(hblocks, slot_index, window_blocks):
    local_blocks = hblocks.shape[0]
    onehot = (slot_index[:, :, None] == jnp.arange(window_blocks)[None, None, :]).astype(jnp.float32)
    hd = jnp.einsum("asp,asij->aipj", onehot, hblocks, precision=HI)
    return hd.reshape(local_blocks * B, window_blocks * B)


def group_exchange(field, groups):
    members = len(groups[0])
    spread = jnp.broadcast_to(field[None], (members,) + field.shape)
    got = lax.all_to_all(spread, "wide", 0, 0, tiled=True, axis_index_groups=groups)
    return got.reshape(members * field.shape[0], field.shape[1])


def apply_ham(field, hdense, groups_a, groups_b):
    got_a = group_exchange(field, groups_a)
    got_b = group_exchange(field, groups_b)
    half = got_a.shape[0]
    return (jnp.dot(hdense[:, :half], got_a, precision=HI, preferred_element_type=jnp.float32)
            + jnp.dot(hdense[:, half:], got_b, precision=HI, preferred_element_type=jnp.float32))


def local(subspace, hblocks, pattern, rotation):
    devcount = lax.axis_size("wide")
    myself = lax.axis_index("wide")
    span = 2 * HW
    groups_a = [[span * k + i for i in range(span)] for k in range(devcount // span)]
    groups_b = [[(span * k + HW + i) % devcount for i in range(span)] for k in range(devcount // span)]
    place = myself % span
    owner = pattern // A_DEV
    offset = (owner - myself + HW + devcount) % devcount - HW
    in_a = (offset + place >= 0) & (offset + place < span)
    piece = jnp.where(in_a, offset + place,
                      span + jnp.where(place < HW, offset + HW + place, offset - HW + place))
    slot_index = piece * A_DEV + pattern % A_DEV
    hdense = dense_hamiltonian(hblocks, slot_index, 2 * span * A_DEV)
    previous = subspace
    current = (apply_ham(subspace, hdense, groups_a, groups_b) - cheb_center * subspace) / cheb_half
    for step in range(DEGREE - 1):
        nextone = (
            2.0 * (apply_ham(current, hdense, groups_a, groups_b) - cheb_center * current) / cheb_half
            - previous
        )
        previous = current
        current = nextone
    total_rows = current.shape[0] * devcount
    gram_term = lax.dot_general(
        current,
        current,
        (((0,), (0,)), ((), ())),
        precision=HI,
        preferred_element_type=jnp.float32,
    )
    pieces = gram_term.reshape(devcount, -1, gram_term.shape[1])
    gathered = lax.all_to_all(pieces, "wide", 0, 0, tiled=True)
    correlation = jnp.sum(gathered, axis=0) / total_rows
    rot_term = jnp.dot(
        current, rotation, precision=HI, preferred_element_type=jnp.float32
    )
    rotated = lax.psum_scatter(rot_term, "grp", scatter_dimension=1, tiled=True)
    return (rotated, correlation)


def solution(mesh):
    in_specs = (P("wide", "grp"), P("wide", None, None, None), P("wide", None), P("grp", None))
    out_specs = (P("wide", "grp"), P(("grp", "wide"), None))
    return jax.shard_map(local, mesh=mesh, in_specs=in_specs, out_specs=out_specs, check_vma=False)
```

```python
import jax
import jax.numpy as jnp
from jax import lax
from jax.experimental import pallas as pl
from jax.experimental.pallas import tpu as pltpu
from jax.sharding import PartitionSpec as P

B = 64
A_DEV = 4
NB = 16
HW = 2
DEGREE = 4


cheb_center = 0.25
cheb_half = 2.0

HI = lax.Precision.HIGHEST


def passed_along(value, axis, steps):
    count = lax.axis_size(axis)
    pairs = [(source, (source + steps) % count) for source in range(count)]
    return lax.ppermute(value, axis, pairs)


def hbuild_kernel(slot_ref, h_ref, o_ref):
    o_ref[...] = jnp.zeros(o_ref.shape, o_ref.dtype)
    for a in range(h_ref.shape[0]):
        for s in range(h_ref.shape[1]):
            p = slot_ref[a, s]
            o_ref[a, p] = o_ref[a, p] + h_ref[a, s]


def dense_hamiltonian(hblocks, slot_index):
    local_blocks = hblocks.shape[0]
    window_blocks = (2 * HW + 1) * A_DEV
    out_bytes = local_blocks * window_blocks * B * B * 4
    hd = pl.pallas_call(
        hbuild_kernel,
        out_shape=jax.ShapeDtypeStruct((local_blocks, window_blocks, B, B), jnp.float32),
        in_specs=[pl.BlockSpec(memory_space=pltpu.SMEM), pl.BlockSpec(memory_space=pltpu.VMEM)],
        out_specs=pl.BlockSpec(memory_space=pltpu.VMEM),
        cost_estimate=pl.CostEstimate(
            flops=hblocks.size, bytes_accessed=hblocks.size * 4 + out_bytes, transcendentals=0
        ),
    )(slot_index, hblocks)
    return hd.transpose(0, 2, 1, 3).reshape(local_blocks * B, window_blocks * B)


def apply_ham(field, hdense):
    rows = field.shape[0]
    pieces = [
        passed_along(field, "wide", 2),
        passed_along(field, "wide", 1),
        field,
        passed_along(field, "wide", -1),
        passed_along(field, "wide", -2),
    ]
    total = None
    for idx in (2, 1, 3, 0, 4):
        term = jnp.dot(hdense[:, idx * rows:(idx + 1) * rows], pieces[idx], precision=HI,
                       preferred_element_type=jnp.float32)
        total = term if total is None else total + term
    return total


def local(subspace, hblocks, pattern, rotation):
    devcount = lax.axis_size("wide")
    myself = lax.axis_index("wide")
    owner = pattern // A_DEV
    relative = (owner - myself + HW + devcount) % devcount
    slot_index = relative * A_DEV + pattern % A_DEV
    hdense = dense_hamiltonian(hblocks, slot_index)
    previous = subspace
    current = (apply_ham(subspace, hdense) - cheb_center * subspace) / cheb_half
    for step in range(DEGREE - 1):
        nextone = (
            2.0 * (apply_ham(current, hdense) - cheb_center * current) / cheb_half
            - previous
        )
        previous = current
        current = nextone
    total_rows = current.shape[0] * devcount
    gram_term = lax.dot_general(
        current,
        current,
        (((0,), (0,)), ((), ())),
        precision=HI,
        preferred_element_type=jnp.float32,
    )
    pieces = gram_term.reshape(devcount, -1, gram_term.shape[1])
    gathered = lax.all_to_all(pieces, "wide", 0, 0, tiled=True)
    correlation = jnp.sum(gathered, axis=0) / total_rows
    rot_term = jnp.dot(
        current, rotation, precision=lax.Precision.HIGH, preferred_element_type=jnp.float32
    )
    rotated = lax.psum_scatter(rot_term, "grp", scatter_dimension=1, tiled=True)
    return (rotated, correlation)


def solution(mesh):
    in_specs = (P("wide", "grp"), P("wide", None, None, None), P("wide", None), P("grp", None))
    out_specs = (P("wide", "grp"), P(("grp", "wide"), None))
    return jax.shard_map(local, mesh=mesh, in_specs=in_specs, out_specs=out_specs, check_vma=False)
```

```python
import jax
import jax.numpy as jnp
from jax import lax
from jax.sharding import PartitionSpec as P

B = 64
A_DEV = 4
NB = 16
HW = 2
DEGREE = 4


cheb_center = 0.25
cheb_half = 2.0

HI = lax.Precision.HIGHEST


def passed_along(value, axis, steps):
    count = lax.axis_size(axis)
    pairs = [(source, (source + steps) % count) for source in range(count)]
    return lax.ppermute(value, axis, pairs)


def dense_hamiltonian(hblocks, slot_index):
    local_blocks = hblocks.shape[0]
    window_blocks = (2 * HW + 1) * A_DEV
    onehot = (slot_index[:, :, None] == jnp.arange(window_blocks)[None, None, :]).astype(jnp.float32)
    hd = jnp.einsum("asp,asij->aipj", onehot, hblocks, precision=HI)
    return hd.reshape(local_blocks * B, window_blocks * B)


def apply_ham(field, hdense, build=None):
    rows = field.shape[0]
    far_up = passed_along(field, "wide", 2)
    far_down = passed_along(field, "wide", -2)
    if build is not None:
        hdense, field = lax.optimization_barrier((build(), field))
    pieces = [
        far_up,
        passed_along(field, "wide", 1),
        field,
        passed_along(field, "wide", -1),
        far_down,
    ]
    total = None
    for idx in (2, 1, 3, 0, 4):
        term = jnp.dot(hdense[:, idx * rows:(idx + 1) * rows], pieces[idx], precision=HI,
                       preferred_element_type=jnp.float32)
        total = term if total is None else total + term
    return total, hdense


def local(subspace, hblocks, pattern, rotation):
    devcount = lax.axis_size("wide")
    myself = lax.axis_index("wide")
    owner = pattern // A_DEV
    relative = (owner - myself + HW + devcount) % devcount
    slot_index = relative * A_DEV + pattern % A_DEV
    previous = subspace
    first, hdense = apply_ham(subspace, None, lambda: dense_hamiltonian(hblocks, slot_index))
    current = (first - cheb_center * subspace) / cheb_half
    for step in range(DEGREE - 1):
        nextone = (
            2.0 * (apply_ham(current, hdense)[0] - cheb_center * current) / cheb_half
            - previous
        )
        previous = current
        current = nextone
    total_rows = current.shape[0] * devcount
    gram_term = lax.dot_general(
        current,
        current,
        (((0,), (0,)), ((), ())),
        precision=HI,
        preferred_element_type=jnp.float32,
    )
    pieces = gram_term.reshape(devcount, -1, gram_term.shape[1])
    gathered = lax.all_to_all(pieces, "wide", 0, 0, tiled=True)
    correlation = jnp.sum(gathered, axis=0) / total_rows
    rot_term = jnp.dot(
        current, rotation, precision=lax.Precision.HIGH, preferred_element_type=jnp.float32
    )
    rotated = lax.psum_scatter(rot_term, "grp", scatter_dimension=1, tiled=True)
    return (rotated, correlation)


def solution(mesh):
    in_specs = (P("wide", "grp"), P("wide", None, None, None), P("wide", None), P("grp", None))
    out_specs = (P("wide", "grp"), P(("grp", "wide"), None))
    return jax.shard_map(local, mesh=mesh, in_specs=in_specs, out_specs=out_specs, check_vma=False)
```

```python
import jax
import jax.numpy as jnp
from jax import lax
from jax.sharding import PartitionSpec as P

B = 64
A_DEV = 4
NB = 16
HW = 2
DEGREE = 4


cheb_center = 0.25
cheb_half = 2.0

HI = lax.Precision.HIGHEST


def passed_along(value, axis, steps):
    count = lax.axis_size(axis)
    pairs = [(source, (source + steps) % count) for source in range(count)]
    return lax.ppermute(value, axis, pairs)


def dense_hamiltonian(hblocks, slot_index):
    local_blocks = hblocks.shape[0]
    window_blocks = (2 * HW + 1) * A_DEV
    onehot = (slot_index[:, :, None] == jnp.arange(window_blocks)[None, None, :]).astype(jnp.bfloat16)
    h1 = lax.reduce_precision(hblocks, exponent_bits=8, mantissa_bits=7)
    rest = hblocks - h1
    h2 = lax.reduce_precision(rest, exponent_bits=8, mantissa_bits=7)
    h3 = rest - h2
    hd = None
    for part in (h3, h2, h1):
        term = jnp.einsum("asp,asij->aipj", onehot, part.astype(jnp.bfloat16),
                          preferred_element_type=jnp.float32)
        hd = term if hd is None else hd + term
    return hd.reshape(local_blocks * B, window_blocks * B)


def apply_ham(field, hdense):
    rows = field.shape[0]
    pieces = [
        passed_along(field, "wide", 2),
        passed_along(field, "wide", 1),
        field,
        passed_along(field, "wide", -1),
        passed_along(field, "wide", -2),
    ]
    total = None
    for idx in (2, 1, 3, 0, 4):
        term = jnp.dot(hdense[:, idx * rows:(idx + 1) * rows], pieces[idx], precision=HI,
                       preferred_element_type=jnp.float32)
        total = term if total is None else total + term
    return total


def local(subspace, hblocks, pattern, rotation):
    devcount = lax.axis_size("wide")
    myself = lax.axis_index("wide")
    owner = pattern // A_DEV
    relative = (owner - myself + HW + devcount) % devcount
    slot_index = relative * A_DEV + pattern % A_DEV
    hdense = dense_hamiltonian(hblocks, slot_index)
    previous = subspace
    current = (apply_ham(subspace, hdense) - cheb_center * subspace) / cheb_half
    for step in range(DEGREE - 1):
        nextone = (
            2.0 * (apply_ham(current, hdense) - cheb_center * current) / cheb_half
            - previous
        )
        previous = current
        current = nextone
    total_rows = current.shape[0] * devcount
    gram_term = lax.dot_general(
        current,
        current,
        (((0,), (0,)), ((), ())),
        precision=HI,
        preferred_element_type=jnp.float32,
    )
    pieces = gram_term.reshape(devcount, -1, gram_term.shape[1])
    gathered = lax.all_to_all(pieces, "wide", 0, 0, tiled=True)
    correlation = jnp.sum(gathered, axis=0) / total_rows
    rot_term = jnp.dot(
        current, rotation, precision=HI, preferred_element_type=jnp.float32
    )
    rotated = lax.psum_scatter(rot_term, "grp", scatter_dimension=1, tiled=True)
    return (rotated, correlation)


def solution(mesh):
    in_specs = (P("wide", "grp"), P("wide", None, None, None), P("wide", None), P("grp", None))
    out_specs = (P("wide", "grp"), P(("grp", "wide"), None))
    return jax.shard_map(local, mesh=mesh, in_specs=in_specs, out_specs=out_specs, check_vma=False)
```

```python
import jax
import jax.numpy as jnp
from jax import lax
from jax.sharding import PartitionSpec as P

B = 64
A_DEV = 4
NB = 16
HW = 2
DEGREE = 4


cheb_center = 0.25
cheb_half = 2.0

HI = lax.Precision.HIGHEST


def passed_along(value, axis, steps):
    count = lax.axis_size(axis)
    pairs = [(source, (source + steps) % count) for source in range(count)]
    return lax.ppermute(value, axis, pairs)


def dense_hamiltonian(hblocks, slot_index):
    local_blocks = hblocks.shape[0]
    window_blocks = (2 * HW + 1) * A_DEV
    onehot = (slot_index[:, :, None] == jnp.arange(window_blocks)[None, None, :]).astype(jnp.float32)
    hd = jnp.einsum("asp,asij->aipj", onehot, hblocks, precision=HI)
    return hd.reshape(local_blocks * B, window_blocks * B)


def apply_ham(field, hdense):
    rows = field.shape[0]
    pieces = [
        passed_along(field, "wide", 2),
        passed_along(field, "wide", 1),
        field,
        passed_along(field, "wide", -1),
        passed_along(field, "wide", -2),
    ]
    total = None
    for idx in (2, 1, 3, 0, 4):
        term = jnp.dot(hdense[:, idx * rows:(idx + 1) * rows], pieces[idx], precision=lax.Precision.HIGH,
                       preferred_element_type=jnp.float32)
        total = term if total is None else total + term
    return total


def local(subspace, hblocks, pattern, rotation):
    devcount = lax.axis_size("wide")
    myself = lax.axis_index("wide")
    owner = pattern // A_DEV
    relative = (owner - myself + HW + devcount) % devcount
    slot_index = relative * A_DEV + pattern % A_DEV
    hdense = dense_hamiltonian(hblocks, slot_index)
    previous = subspace
    current = (apply_ham(subspace, hdense) - cheb_center * subspace) / cheb_half
    for step in range(DEGREE - 1):
        nextone = (
            2.0 * (apply_ham(current, hdense) - cheb_center * current) / cheb_half
            - previous
        )
        previous = current
        current = nextone
    total_rows = current.shape[0] * devcount
    gram_term = lax.dot_general(
        current,
        current,
        (((0,), (0,)), ((), ())),
        precision=HI,
        preferred_element_type=jnp.float32,
    )
    pieces = gram_term.reshape(devcount, -1, gram_term.shape[1])
    gathered = lax.all_to_all(pieces, "wide", 0, 0, tiled=True)
    correlation = jnp.sum(gathered, axis=0) / total_rows
    rot_term = jnp.dot(
        current, rotation, precision=lax.Precision.HIGH, preferred_element_type=jnp.float32
    )
    rotated = lax.psum_scatter(rot_term, "grp", scatter_dimension=1, tiled=True)
    return (rotated, correlation)


def solution(mesh):
    in_specs = (P("wide", "grp"), P("wide", None, None, None), P("wide", None), P("grp", None))
    out_specs = (P("wide", "grp"), P(("grp", "wide"), None))
    return jax.shard_map(local, mesh=mesh, in_specs=in_specs, out_specs=out_specs, check_vma=False)
```

```python
import jax
import jax.numpy as jnp
from jax import lax
from jax.sharding import PartitionSpec as P

B = 64
A_DEV = 4
NB = 16
HW = 2
DEGREE = 4


cheb_center = 0.25
cheb_half = 2.0

HI = lax.Precision.HIGHEST


def passed_along(value, axis, steps):
    count = lax.axis_size(axis)
    pairs = [(source, (source + steps) % count) for source in range(count)]
    return lax.ppermute(value, axis, pairs)


def dense_hamiltonian(hblocks, slot_index):
    local_blocks = hblocks.shape[0]
    window_blocks = (2 * HW + 1) * A_DEV
    slots = hblocks.shape[1]
    hits = slot_index[:, :, None] == jnp.arange(window_blocks)[None, None, :]
    same = jnp.eye(local_blocks, dtype=bool)
    select = (jnp.transpose(hits, (0, 2, 1))[:, :, None, :] & same[:, None, :, None]).astype(jnp.float32)
    select = select.reshape(local_blocks * window_blocks, local_blocks * slots)
    hd = jnp.dot(select, hblocks.reshape(local_blocks * slots, B * B), precision=HI,
                 preferred_element_type=jnp.float32)
    hd = hd.reshape(local_blocks, window_blocks, B, B).transpose(0, 2, 1, 3)
    return hd.reshape(local_blocks * B, window_blocks * B)


def apply_ham(field, hdense):
    rows = field.shape[0]
    pieces = [
        passed_along(field, "wide", 2),
        passed_along(field, "wide", 1),
        field,
        passed_along(field, "wide", -1),
        passed_along(field, "wide", -2),
    ]
    total = None
    for idx in (2, 1, 3, 0, 4):
        term = jnp.dot(hdense[:, idx * rows:(idx + 1) * rows], pieces[idx], precision=HI,
                       preferred_element_type=jnp.float32)
        total = term if total is None else total + term
    return total


def local(subspace, hblocks, pattern, rotation):
    devcount = lax.axis_size("wide")
    myself = lax.axis_index("wide")
    owner = pattern // A_DEV
    relative = (owner - myself + HW + devcount) % devcount
    slot_index = relative * A_DEV + pattern % A_DEV
    hdense = dense_hamiltonian(hblocks, slot_index)
    previous = subspace
    current = (apply_ham(subspace, hdense) - cheb_center * subspace) / cheb_half
    for step in range(DEGREE - 1):
        nextone = (
            2.0 * (apply_ham(current, hdense) - cheb_center * current) / cheb_half
            - previous
        )
        previous = current
        current = nextone
    total_rows = current.shape[0] * devcount
    gram_term = lax.dot_general(
        current,
        current,
        (((0,), (0,)), ((), ())),
        precision=HI,
        preferred_element_type=jnp.float32,
    )
    pieces = gram_term.reshape(devcount, -1, gram_term.shape[1])
    gathered = lax.all_to_all(pieces, "wide", 0, 0, tiled=True)
    correlation = jnp.sum(gathered, axis=0) / total_rows
    rot_term = jnp.dot(
        current, rotation, precision=HI, preferred_element_type=jnp.float32
    )
    rotated = lax.psum_scatter(rot_term, "grp", scatter_dimension=1, tiled=True)
    return (rotated, correlation)


def solution(mesh):
    in_specs = (P("wide", "grp"), P("wide", None, None, None), P("wide", None), P("grp", None))
    out_specs = (P("wide", "grp"), P(("grp", "wide"), None))
    return jax.shard_map(local, mesh=mesh, in_specs=in_specs, out_specs=out_specs, check_vma=False)
```

```python
import jax
import jax.numpy as jnp
from jax import lax
from jax.sharding import PartitionSpec as P

B = 64
A_DEV = 4
NB = 16
HW = 2
DEGREE = 4


cheb_center = 0.25
cheb_half = 2.0

HI = lax.Precision.HIGHEST


def passed_along(value, axis, steps):
    count = lax.axis_size(axis)
    pairs = [(source, (source + steps) % count) for source in range(count)]
    return lax.ppermute(value, axis, pairs)


def dense_hamiltonian(hblocks, slot_index):
    local_blocks = hblocks.shape[0]
    window_blocks = (2 * HW + 1) * A_DEV
    onehot = (slot_index[:, :, None] == jnp.arange(window_blocks)[None, None, :]).astype(jnp.float32)
    hd = jnp.einsum("asp,asij->aipj", onehot, hblocks, precision=HI)
    return hd.reshape(local_blocks * B, window_blocks * B)


def apply_ham(field, hdense):
    rows = field.shape[0]
    pieces = [
        passed_along(field, "wide", 2),
        passed_along(field, "wide", 1),
        field,
        passed_along(field, "wide", -1),
        passed_along(field, "wide", -2),
    ]
    total = None
    for idx in (2, 1, 3, 0, 4):
        term = jnp.dot(hdense[:, idx * rows:(idx + 1) * rows], pieces[idx], precision=HI,
                       preferred_element_type=jnp.float32)
        total = term if total is None else total + term
    return total


def local(subspace, hblocks, pattern, rotation):
    devcount = lax.axis_size("wide")
    myself = lax.axis_index("wide")
    owner = pattern // A_DEV
    relative = (owner - myself + HW + devcount) % devcount
    slot_index = relative * A_DEV + pattern % A_DEV
    local_blocks = hblocks.shape[0]
    shift = jnp.broadcast_to(-cheb_center * jnp.eye(B, dtype=jnp.float32), (local_blocks, 1, B, B))
    blocks_ext = (2.0 / cheb_half) * jnp.concatenate([hblocks, shift], axis=1)
    self_slot = HW * A_DEV + jnp.arange(local_blocks, dtype=slot_index.dtype)[:, None]
    hdense = dense_hamiltonian(blocks_ext, jnp.concatenate([slot_index, self_slot], axis=1))
    rows = subspace.shape[0]
    step_op = hdense
    previous = subspace
    current = 0.5 * apply_ham(subspace, step_op)
    for step in range(DEGREE - 1):
        nextone = apply_ham(current, step_op) - previous
        previous = current
        current = nextone
    total_rows = current.shape[0] * devcount
    gram_term = lax.dot_general(
        current,
        current,
        (((0,), (0,)), ((), ())),
        precision=HI,
        preferred_element_type=jnp.float32,
    )
    pieces = gram_term.reshape(devcount, -1, gram_term.shape[1])
    gathered = lax.all_to_all(pieces, "wide", 0, 0, tiled=True)
    correlation = jnp.sum(gathered, axis=0) / total_rows
    rot_term = jnp.dot(
        current, rotation, precision=HI, preferred_element_type=jnp.float32
    )
    rotated = lax.psum_scatter(rot_term, "grp", scatter_dimension=1, tiled=True)
    return (rotated, correlation)


def solution(mesh):
    in_specs = (P("wide", "grp"), P("wide", None, None, None), P("wide", None), P("grp", None))
    out_specs = (P("wide", "grp"), P(("grp", "wide"), None))
    return jax.shard_map(local, mesh=mesh, in_specs=in_specs, out_specs=out_specs, check_vma=False)
```

```python
import jax
import jax.numpy as jnp
from jax import lax
from jax.sharding import PartitionSpec as P

B = 64
A_DEV = 4
NB = 16
HW = 2
DEGREE = 4


cheb_center = 0.25
cheb_half = 2.0

HI = lax.Precision.HIGHEST


def passed_along(value, axis, steps):
    count = lax.axis_size(axis)
    pairs = [(source, (source + steps) % count) for source in range(count)]
    return lax.ppermute(value, axis, pairs)


def dense_hamiltonian(hblocks, slot_index):
    local_blocks = hblocks.shape[0]
    window_blocks = (2 * HW + 1) * A_DEV
    onehot = (slot_index[:, :, None] == jnp.arange(window_blocks)[None, None, :]).astype(jnp.float32)
    hd = jnp.einsum("asp,asij->aipj", onehot, hblocks, precision=HI)
    return hd.reshape(local_blocks * B, window_blocks * B)


def apply_ham(field, hdense):
    rows = field.shape[0]
    count = lax.axis_size("wide")
    swap_pairs = [(i, i ^ 1) for i in range(count)]
    cross_pairs = [(i, (i - 1) % count if i % 2 == 0 else (i + 1) % count) for i in range(count)]
    pieces = [
        passed_along(field, "wide", 2),
        lax.ppermute(field, "wide", swap_pairs),
        field,
        lax.ppermute(field, "wide", cross_pairs),
        passed_along(field, "wide", -2),
    ]
    total = None
    for idx in (2, 1, 3, 0, 4):
        term = jnp.dot(hdense[:, idx * rows:(idx + 1) * rows], pieces[idx], precision=HI,
                       preferred_element_type=jnp.float32)
        total = term if total is None else total + term
    return total


def local(subspace, hblocks, pattern, rotation):
    devcount = lax.axis_size("wide")
    myself = lax.axis_index("wide")
    owner = pattern // A_DEV
    relative = (owner - myself + HW + devcount) % devcount
    relative = jnp.where(myself % 2 == 0, jnp.where(relative == 1, 3, jnp.where(relative == 3, 1, relative)), relative)
    slot_index = relative * A_DEV + pattern % A_DEV
    hdense = dense_hamiltonian(hblocks, slot_index)
    previous = subspace
    current = (apply_ham(subspace, hdense) - cheb_center * subspace) / cheb_half
    for step in range(DEGREE - 1):
        nextone = (
            2.0 * (apply_ham(current, hdense) - cheb_center * current) / cheb_half
            - previous
        )
        previous = current
        current = nextone
    total_rows = current.shape[0] * devcount
    gram_term = lax.dot_general(
        current,
        current,
        (((0,), (0,)), ((), ())),
        precision=HI,
        preferred_element_type=jnp.float32,
    )
    pieces = gram_term.reshape(devcount, -1, gram_term.shape[1])
    gathered = lax.all_to_all(pieces, "wide", 0, 0, tiled=True)
    correlation = jnp.sum(gathered, axis=0) / total_rows
    rot_term = jnp.dot(
        current, rotation, precision=HI, preferred_element_type=jnp.float32
    )
    rotated = lax.psum_scatter(rot_term, "grp", scatter_dimension=1, tiled=True)
    return (rotated, correlation)


def solution(mesh):
    in_specs = (P("wide", "grp"), P("wide", None, None, None), P("wide", None), P("grp", None))
    out_specs = (P("wide", "grp"), P(("grp", "wide"), None))
    return jax.shard_map(local, mesh=mesh, in_specs=in_specs, out_specs=out_specs, check_vma=False)
```

```python
import jax
import jax.numpy as jnp
from jax import lax
from jax.sharding import PartitionSpec as P

B = 64
A_DEV = 4
NB = 16
HW = 2
DEGREE = 4


cheb_center = 0.25
cheb_half = 2.0

HI = lax.Precision.HIGHEST


def passed_along(value, axis, steps):
    count = lax.axis_size(axis)
    pairs = [(source, (source + steps) % count) for source in range(count)]
    return lax.ppermute(value, axis, pairs)


def dense_hamiltonian(hblocks, slot_index):
    local_blocks = hblocks.shape[0]
    window_blocks = (2 * HW + 1) * A_DEV
    onehot = (slot_index[:, :, None] == jnp.arange(window_blocks)[None, None, :]).astype(jnp.float32)
    hd = jnp.einsum("asp,asij->aipj", onehot, hblocks, precision=HI)
    return hd.reshape(local_blocks * B, window_blocks * B)


def apply_ham(field, hdense):
    rows = field.shape[0]
    count = lax.axis_size("wide")
    swap_pairs = [(i, i ^ 1) for i in range(count)]
    cross_pairs = [(i, (i - 1) % count if i % 2 == 0 else (i + 1) % count) for i in range(count)]
    near_pairs = [(i, (i + 2) % count if (i // 2) % 2 == 0 else (i - 2) % count) for i in range(count)]
    wrap_pairs = [(i, (i - 2) % count if (i // 2) % 2 == 0 else (i + 2) % count) for i in range(count)]
    pieces = [
        lax.ppermute(field, "wide", near_pairs),
        lax.ppermute(field, "wide", swap_pairs),
        field,
        lax.ppermute(field, "wide", cross_pairs),
        lax.ppermute(field, "wide", wrap_pairs),
    ]
    total = None
    for idx in (2, 1, 3, 0, 4):
        term = jnp.dot(hdense[:, idx * rows:(idx + 1) * rows], pieces[idx], precision=HI,
                       preferred_element_type=jnp.float32)
        total = term if total is None else total + term
    return total


def local(subspace, hblocks, pattern, rotation):
    devcount = lax.axis_size("wide")
    myself = lax.axis_index("wide")
    owner = pattern // A_DEV
    relative = (owner - myself + HW + devcount) % devcount
    relative = jnp.where(myself % 2 == 0, jnp.where(relative == 1, 3, jnp.where(relative == 3, 1, relative)), relative)
    relative = jnp.where((myself // 2) % 2 == 0, jnp.where(relative == 0, 4, jnp.where(relative == 4, 0, relative)), relative)
    slot_index = relative * A_DEV + pattern % A_DEV
    hdense = dense_hamiltonian(hblocks, slot_index)
    previous = subspace
    current = (apply_ham(subspace, hdense) - cheb_center * subspace) / cheb_half
    for step in range(DEGREE - 1):
        nextone = (
            2.0 * (apply_ham(current, hdense) - cheb_center * current) / cheb_half
            - previous
        )
        previous = current
        current = nextone
    total_rows = current.shape[0] * devcount
    gram_term = lax.dot_general(
        current,
        current,
        (((0,), (0,)), ((), ())),
        precision=HI,
        preferred_element_type=jnp.float32,
    )
    pieces = gram_term.reshape(devcount, -1, gram_term.shape[1])
    gathered = lax.all_to_all(pieces, "wide", 0, 0, tiled=True)
    correlation = jnp.sum(gathered, axis=0) / total_rows
    rot_term = jnp.dot(
        current, rotation, precision=HI, preferred_element_type=jnp.float32
    )
    rotated = lax.psum_scatter(rot_term, "grp", scatter_dimension=1, tiled=True)
    return (rotated, correlation)


def solution(mesh):
    in_specs = (P("wide", "grp"), P("wide", None, None, None), P("wide", None), P("grp", None))
    out_specs = (P("wide", "grp"), P(("grp", "wide"), None))
    return jax.shard_map(local, mesh=mesh, in_specs=in_specs, out_specs=out_specs, check_vma=False)
```

```python
import jax
import jax.numpy as jnp
from jax import lax
from jax.sharding import PartitionSpec as P

B = 64
A_DEV = 4
NB = 16
HW = 2
DEGREE = 4


cheb_center = 0.25
cheb_half = 2.0

HI = lax.Precision.HIGHEST


def passed_along(value, axis, steps):
    count = lax.axis_size(axis)
    pairs = [(source, (source + steps) % count) for source in range(count)]
    return lax.ppermute(value, axis, pairs)


def dense_hamiltonian(hblocks, slot_index):
    local_blocks = hblocks.shape[0]
    window_blocks = (2 * HW + 1) * A_DEV
    onehot = (slot_index[:, :, None] == jnp.arange(window_blocks)[None, None, :]).astype(jnp.float32)
    hd = jnp.einsum("asp,asij->aipj", onehot, hblocks, precision=HI)
    return hd.reshape(local_blocks * B, window_blocks * B)


def apply_ham(field, hdense):
    rows = field.shape[0]
    count = lax.axis_size("wide")
    swap_pairs = [(i, i ^ 1) for i in range(count)]
    cross_pairs = [(i, (i - 1) % count if i % 2 == 0 else (i + 1) % count) for i in range(count)]
    near_pairs = [(i, (i + 2) % count if (i // 2) % 2 == 0 else (i - 2) % count) for i in range(count)]
    wrap_pairs = [(i, (i - 2) % count if (i // 2) % 2 == 0 else (i + 2) % count) for i in range(count)]
    pieces = [
        lax.ppermute(field, "wide", near_pairs),
        lax.ppermute(field, "wide", swap_pairs),
        field,
        lax.ppermute(field, "wide", cross_pairs),
        lax.ppermute(field, "wide", wrap_pairs),
    ]
    total = None
    for idx in (2, 1, 3, 0, 4):
        term = jnp.dot(hdense[:, idx * rows:(idx + 1) * rows], pieces[idx], precision=HI,
                       preferred_element_type=jnp.float32)
        total = term if total is None else total + term
    return total


def local(subspace, hblocks, pattern, rotation):
    devcount = lax.axis_size("wide")
    myself = lax.axis_index("wide")
    owner = pattern // A_DEV
    relative = (owner - myself + HW + devcount) % devcount
    relative = jnp.where(myself % 2 == 0, jnp.where(relative == 1, 3, jnp.where(relative == 3, 1, relative)), relative)
    relative = jnp.where((myself // 2) % 2 == 0, jnp.where(relative == 0, 4, jnp.where(relative == 4, 0, relative)), relative)
    slot_index = relative * A_DEV + pattern % A_DEV
    hdense = dense_hamiltonian(hblocks, slot_index)
    subspace, probe_h = lax.optimization_barrier((subspace, hdense[:8, :128]))
    subspace = subspace + 0.0 * probe_h[0, 0]
    previous = subspace
    current = (apply_ham(subspace, hdense) - cheb_center * subspace) / cheb_half
    for step in range(DEGREE - 1):
        nextone = (
            2.0 * (apply_ham(current, hdense) - cheb_center * current) / cheb_half
            - previous
        )
        previous = current
        current = nextone
    total_rows = current.shape[0] * devcount
    gram_term = lax.dot_general(
        current,
        current,
        (((0,), (0,)), ((), ())),
        precision=HI,
        preferred_element_type=jnp.float32,
    )
    pieces = gram_term.reshape(devcount, -1, gram_term.shape[1])
    gathered = lax.all_to_all(pieces, "wide", 0, 0, tiled=True)
    correlation = jnp.sum(gathered, axis=0) / total_rows
    rot_term = jnp.dot(
        current, rotation, precision=HI, preferred_element_type=jnp.float32
    )
    rotated = lax.psum_scatter(rot_term, "grp", scatter_dimension=1, tiled=True)
    return (rotated, correlation)


def solution(mesh):
    in_specs = (P("wide", "grp"), P("wide", None, None, None), P("wide", None), P("grp", None))
    out_specs = (P("wide", "grp"), P(("grp", "wide"), None))
    return jax.shard_map(local, mesh=mesh, in_specs=in_specs, out_specs=out_specs, check_vma=False)
```

```python
import jax
import jax.numpy as jnp
from jax import lax
from jax.sharding import PartitionSpec as P

B = 64
A_DEV = 4
NB = 16
HW = 2
DEGREE = 4


cheb_center = 0.25
cheb_half = 2.0

HI = lax.Precision.HIGHEST


def passed_along(value, axis, steps):
    count = lax.axis_size(axis)
    pairs = [(source, (source + steps) % count) for source in range(count)]
    return lax.ppermute(value, axis, pairs)


def dense_hamiltonian(hblocks, slot_index):
    local_blocks = hblocks.shape[0]
    window_blocks = (2 * HW + 1) * A_DEV
    onehot = (slot_index[:, :, None] == jnp.arange(window_blocks)[None, None, :]).astype(jnp.float32)
    hd = jnp.einsum("asp,asij->aipj", onehot, hblocks, precision=HI)
    return hd.reshape(local_blocks * B, window_blocks * B)


def apply_ham(field, hdense):
    rows = field.shape[0]
    count = lax.axis_size("wide")
    swap_pairs = [(i, i ^ 1) for i in range(count)]
    cross_pairs = [(i, (i - 1) % count if i % 2 == 0 else (i + 1) % count) for i in range(count)]
    near_pairs = [(i, (i + 2) % count if (i // 2) % 2 == 0 else (i - 2) % count) for i in range(count)]
    wrap_pairs = [(i, (i - 2) % count if (i // 2) % 2 == 0 else (i + 2) % count) for i in range(count)]
    pieces = [
        lax.ppermute(field, "wide", near_pairs),
        lax.ppermute(field, "wide", swap_pairs),
        field,
        lax.ppermute(field, "wide", cross_pairs),
        lax.ppermute(field, "wide", wrap_pairs),
    ]
    total = None
    for idx in (2, 1, 3, 0, 4):
        term = jnp.dot(hdense[:, idx * rows:(idx + 1) * rows], pieces[idx], precision=HI,
                       preferred_element_type=jnp.float32)
        total = term if total is None else total + term
    return total


def split3(x):
    x1 = lax.reduce_precision(x, exponent_bits=8, mantissa_bits=7)
    rest = x - x1
    x2 = lax.reduce_precision(rest, exponent_bits=8, mantissa_bits=7)
    return [p.astype(jnp.bfloat16) for p in (x1, x2, rest - x2)]


def split_dot(a, b_parts):
    a_parts = split3(a)
    total = None
    for i, j in ((1, 1), (2, 0), (0, 2), (1, 0), (0, 1), (0, 0)):
        term = jnp.dot(a_parts[i], b_parts[j], preferred_element_type=jnp.float32)
        total = term if total is None else total + term
    return total


def local(subspace, hblocks, pattern, rotation):
    devcount = lax.axis_size("wide")
    myself = lax.axis_index("wide")
    owner = pattern // A_DEV
    relative = (owner - myself + HW + devcount) % devcount
    relative = jnp.where(myself % 2 == 0, jnp.where(relative == 1, 3, jnp.where(relative == 3, 1, relative)), relative)
    relative = jnp.where((myself // 2) % 2 == 0, jnp.where(relative == 0, 4, jnp.where(relative == 4, 0, relative)), relative)
    slot_index = relative * A_DEV + pattern % A_DEV
    hdense = dense_hamiltonian(hblocks, slot_index)
    subspace, probe_h = lax.optimization_barrier((subspace, hdense[:8, :128]))
    subspace = subspace + 0.0 * probe_h[0, 0]
    previous = subspace
    current = (apply_ham(subspace, hdense) - cheb_center * subspace) / cheb_half
    for step in range(DEGREE - 1):
        nextone = (
            2.0 * (apply_ham(current, hdense) - cheb_center * current) / cheb_half
            - previous
        )
        previous = current
        current = nextone
    total_rows = current.shape[0] * devcount
    gram_term = lax.dot_general(
        current,
        current,
        (((0,), (0,)), ((), ())),
        precision=HI,
        preferred_element_type=jnp.float32,
    )
    pieces = gram_term.reshape(devcount, -1, gram_term.shape[1])
    gathered = lax.all_to_all(pieces, "wide", 0, 0, tiled=True)
    correlation = jnp.sum(gathered, axis=0) / total_rows
    rot_term = split_dot(current, split3(rotation))
    rotated = lax.psum_scatter(rot_term, "grp", scatter_dimension=1, tiled=True)
    return (rotated, correlation)


def solution(mesh):
    in_specs = (P("wide", "grp"), P("wide", None, None, None), P("wide", None), P("grp", None))
    out_specs = (P("wide", "grp"), P(("grp", "wide"), None))
    return jax.shard_map(local, mesh=mesh, in_specs=in_specs, out_specs=out_specs, check_vma=False)
```

```python
import jax
import jax.numpy as jnp
from jax import lax
from jax.sharding import PartitionSpec as P

B = 64
A_DEV = 4
NB = 16
HW = 2
DEGREE = 4


cheb_center = 0.25
cheb_half = 2.0

HI = lax.Precision.HIGHEST


def passed_along(value, axis, steps):
    count = lax.axis_size(axis)
    pairs = [(source, (source + steps) % count) for source in range(count)]
    return lax.ppermute(value, axis, pairs)


def dense_hamiltonian(hblocks, slot_index):
    local_blocks = hblocks.shape[0]
    window_blocks = (2 * HW + 1) * A_DEV
    onehot = (slot_index[:, :, None] == jnp.arange(window_blocks)[None, None, :]).astype(jnp.float32)
    hd = jnp.einsum("asp,asij->aipj", onehot, hblocks, precision=HI)
    return hd.reshape(local_blocks * B, window_blocks * B)


def apply_ham(field, hdense):
    rows = field.shape[0]
    count = lax.axis_size("wide")
    swap_pairs = [(i, i ^ 1) for i in range(count)]
    cross_pairs = [(i, (i - 1) % count if i % 2 == 0 else (i + 1) % count) for i in range(count)]
    near_pairs = [(i, (i + 2) % count if (i // 2) % 2 == 0 else (i - 2) % count) for i in range(count)]
    wrap_pairs = [(i, (i - 2) % count if (i // 2) % 2 == 0 else (i + 2) % count) for i in range(count)]
    pieces = [
        lax.ppermute(field, "wide", near_pairs),
        lax.ppermute(field, "wide", swap_pairs),
        field,
        lax.ppermute(field, "wide", cross_pairs),
        lax.ppermute(field, "wide", wrap_pairs),
    ]
    total = None
    for idx in (2, 1, 3, 0, 4):
        term = jnp.dot(hdense[:, idx * rows:(idx + 1) * rows], pieces[idx], precision=HI,
                       preferred_element_type=jnp.float32)
        total = term if total is None else total + term
    return total


def local(subspace, hblocks, pattern, rotation):
    devcount = lax.axis_size("wide")
    myself = lax.axis_index("wide")
    owner = pattern // A_DEV
    relative = (owner - myself + HW + devcount) % devcount
    relative = jnp.where(myself % 2 == 0, jnp.where(relative == 1, 3, jnp.where(relative == 3, 1, relative)), relative)
    relative = jnp.where((myself // 2) % 2 == 0, jnp.where(relative == 0, 4, jnp.where(relative == 4, 0, relative)), relative)
    slot_index = relative * A_DEV + pattern % A_DEV
    hdense = dense_hamiltonian(hblocks, slot_index)
    subspace, probe_h = lax.optimization_barrier((subspace, hdense[:8, :128]))
    previous = subspace
    current = (apply_ham(subspace, hdense) - cheb_center * subspace) / cheb_half
    for step in range(DEGREE - 1):
        nextone = (
            2.0 * (apply_ham(current, hdense) - cheb_center * current) / cheb_half
            - previous
        )
        previous = current
        current = nextone
    total_rows = current.shape[0] * devcount
    gram_term = lax.dot_general(
        current,
        current,
        (((0,), (0,)), ((), ())),
        precision=HI,
        preferred_element_type=jnp.float32,
    )
    pieces = gram_term.reshape(devcount, -1, gram_term.shape[1])
    gathered = lax.all_to_all(pieces, "wide", 0, 0, tiled=True)
    correlation = jnp.sum(gathered, axis=0) / total_rows + 0.0 * probe_h[0, 0]
    rot_term = jnp.dot(
        current, rotation, precision=HI, preferred_element_type=jnp.float32
    )
    rotated = lax.psum_scatter(rot_term, "grp", scatter_dimension=1, tiled=True)
    return (rotated, correlation)


def solution(mesh):
    in_specs = (P("wide", "grp"), P("wide", None, None, None), P("wide", None), P("grp", None))
    out_specs = (P("wide", "grp"), P(("grp", "wide"), None))
    return jax.shard_map(local, mesh=mesh, in_specs=in_specs, out_specs=out_specs, check_vma=False)
```

```python
import jax
import jax.numpy as jnp
from jax import lax
from jax.sharding import PartitionSpec as P

B = 64
A_DEV = 4
NB = 16
HW = 2
DEGREE = 4


cheb_center = 0.25
cheb_half = 2.0

HI = lax.Precision.HIGHEST


def passed_along(value, axis, steps):
    count = lax.axis_size(axis)
    pairs = [(source, (source + steps) % count) for source in range(count)]
    return lax.ppermute(value, axis, pairs)


def dense_hamiltonian(hblocks, slot_index):
    local_blocks = hblocks.shape[0]
    window_blocks = (2 * HW + 1) * A_DEV
    onehot = (slot_index[:, :, None] == jnp.arange(window_blocks)[None, None, :]).astype(jnp.float32)
    hd = jnp.einsum("asp,asij->aipj", onehot, hblocks, precision=HI)
    return hd.reshape(local_blocks * B, window_blocks * B), hd[0, :8, 0, :]


def apply_ham(field, hdense):
    rows = field.shape[0]
    count = lax.axis_size("wide")
    swap_pairs = [(i, i ^ 1) for i in range(count)]
    cross_pairs = [(i, (i - 1) % count if i % 2 == 0 else (i + 1) % count) for i in range(count)]
    near_pairs = [(i, (i + 2) % count if (i // 2) % 2 == 0 else (i - 2) % count) for i in range(count)]
    wrap_pairs = [(i, (i - 2) % count if (i // 2) % 2 == 0 else (i + 2) % count) for i in range(count)]
    pieces = [
        lax.ppermute(field, "wide", near_pairs),
        lax.ppermute(field, "wide", swap_pairs),
        field,
        lax.ppermute(field, "wide", cross_pairs),
        lax.ppermute(field, "wide", wrap_pairs),
    ]
    total = None
    for idx in (2, 1, 3, 0, 4):
        term = jnp.dot(hdense[:, idx * rows:(idx + 1) * rows], pieces[idx], precision=HI,
                       preferred_element_type=jnp.float32)
        total = term if total is None else total + term
    return total


def local(subspace, hblocks, pattern, rotation):
    devcount = lax.axis_size("wide")
    myself = lax.axis_index("wide")
    owner = pattern // A_DEV
    relative = (owner - myself + HW + devcount) % devcount
    relative = jnp.where(myself % 2 == 0, jnp.where(relative == 1, 3, jnp.where(relative == 3, 1, relative)), relative)
    relative = jnp.where((myself // 2) % 2 == 0, jnp.where(relative == 0, 4, jnp.where(relative == 4, 0, relative)), relative)
    slot_index = relative * A_DEV + pattern % A_DEV
    hdense, probe_h = dense_hamiltonian(hblocks, slot_index)
    subspace, probe_h = lax.optimization_barrier((subspace, probe_h))
    previous = subspace
    current = (apply_ham(subspace, hdense) - cheb_center * subspace) / cheb_half
    for step in range(DEGREE - 1):
        nextone = (
            2.0 * (apply_ham(current, hdense) - cheb_center * current) / cheb_half
            - previous
        )
        previous = current
        current = nextone
    total_rows = current.shape[0] * devcount
    gram_term = lax.dot_general(
        current,
        current,
        (((0,), (0,)), ((), ())),
        precision=HI,
        preferred_element_type=jnp.float32,
    )
    pieces = gram_term.reshape(devcount, -1, gram_term.shape[1])
    gathered = lax.all_to_all(pieces, "wide", 0, 0, tiled=True)
    correlation = jnp.sum(gathered, axis=0) / total_rows + 0.0 * probe_h[0, 0]
    rot_term = jnp.dot(
        current, rotation, precision=HI, preferred_element_type=jnp.float32
    )
    rotated = lax.psum_scatter(rot_term, "grp", scatter_dimension=1, tiled=True)
    return (rotated, correlation)


def solution(mesh):
    in_specs = (P("wide", "grp"), P("wide", None, None, None), P("wide", None), P("grp", None))
    out_specs = (P("wide", "grp"), P(("grp", "wide"), None))
    return jax.shard_map(local, mesh=mesh, in_specs=in_specs, out_specs=out_specs, check_vma=False)
```

```python
import jax
import jax.numpy as jnp
from jax import lax
from jax.sharding import PartitionSpec as P

B = 64
A_DEV = 4
NB = 16
HW = 2
DEGREE = 4


cheb_center = 0.25
cheb_half = 2.0

HI = lax.Precision.HIGHEST


def passed_along(value, axis, steps):
    count = lax.axis_size(axis)
    pairs = [(source, (source + steps) % count) for source in range(count)]
    return lax.ppermute(value, axis, pairs)


def dense_hamiltonian(hblocks, slot_index):
    local_blocks = hblocks.shape[0]
    window_blocks = (2 * HW + 1) * A_DEV
    onehot = (slot_index[:, :, None] == jnp.arange(window_blocks)[None, None, :]).astype(jnp.float32)
    hd = jnp.einsum("asp,asij->aipj", onehot, hblocks, precision=HI)
    return hd.reshape(local_blocks * B, window_blocks * B)


def apply_ham(field, hdense):
    rows = field.shape[0]
    count = lax.axis_size("wide")
    swap_pairs = [(i, i ^ 1) for i in range(count)]
    cross_pairs = [(i, (i - 1) % count if i % 2 == 0 else (i + 1) % count) for i in range(count)]
    near_pairs = [(i, (i + 2) % count if (i // 2) % 2 == 0 else (i - 2) % count) for i in range(count)]
    wrap_pairs = [(i, (i - 2) % count if (i // 2) % 2 == 0 else (i + 2) % count) for i in range(count)]
    pieces = [
        lax.ppermute(field, "wide", near_pairs),
        lax.ppermute(field, "wide", swap_pairs),
        field,
        lax.ppermute(field, "wide", cross_pairs),
        lax.ppermute(field, "wide", wrap_pairs),
    ]
    total = None
    for idx in (2, 1, 0, 3, 4):
        term = jnp.dot(hdense[:, idx * rows:(idx + 1) * rows], pieces[idx], precision=HI,
                       preferred_element_type=jnp.float32)
        total = term if total is None else total + term
    return total


def local(subspace, hblocks, pattern, rotation):
    devcount = lax.axis_size("wide")
    myself = lax.axis_index("wide")
    owner = pattern // A_DEV
    relative = (owner - myself + HW + devcount) % devcount
    relative = jnp.where(myself % 2 == 0, jnp.where(relative == 1, 3, jnp.where(relative == 3, 1, relative)), relative)
    relative = jnp.where((myself // 2) % 2 == 0, jnp.where(relative == 0, 4, jnp.where(relative == 4, 0, relative)), relative)
    slot_index = relative * A_DEV + pattern % A_DEV
    hdense = dense_hamiltonian(hblocks, slot_index)
    subspace, probe_h = lax.optimization_barrier((subspace, hdense[:8, :128]))
    previous = subspace
    current = (apply_ham(subspace, hdense) - cheb_center * subspace) / cheb_half
    for step in range(DEGREE - 1):
        nextone = (
            2.0 * (apply_ham(current, hdense) - cheb_center * current) / cheb_half
            - previous
        )
        previous = current
        current = nextone
    total_rows = current.shape[0] * devcount
    gram_term = lax.dot_general(
        current,
        current,
        (((0,), (0,)), ((), ())),
        precision=HI,
        preferred_element_type=jnp.float32,
    )
    pieces = gram_term.reshape(devcount, -1, gram_term.shape[1])
    gathered = lax.all_to_all(pieces, "wide", 0, 0, tiled=True)
    correlation = jnp.sum(gathered, axis=0) / total_rows + 0.0 * probe_h[0, 0]
    rot_term = jnp.dot(
        current, rotation, precision=HI, preferred_element_type=jnp.float32
    )
    rotated = lax.psum_scatter(rot_term, "grp", scatter_dimension=1, tiled=True)
    return (rotated, correlation)


def solution(mesh):
    in_specs = (P("wide", "grp"), P("wide", None, None, None), P("wide", None), P("grp", None))
    out_specs = (P("wide", "grp"), P(("grp", "wide"), None))
    return jax.shard_map(local, mesh=mesh, in_specs=in_specs, out_specs=out_specs, check_vma=False)
```

```python
import jax
import jax.numpy as jnp
from jax import lax
from jax.sharding import PartitionSpec as P

B = 64
A_DEV = 4
NB = 16
HW = 2
DEGREE = 4


cheb_center = 0.25
cheb_half = 2.0

HI = lax.Precision.HIGHEST


def passed_along(value, axis, steps):
    count = lax.axis_size(axis)
    pairs = [(source, (source + steps) % count) for source in range(count)]
    return lax.ppermute(value, axis, pairs)


def dense_hamiltonian(hblocks, slot_index):
    local_blocks = hblocks.shape[0]
    window_blocks = (2 * HW + 1) * A_DEV
    onehot = (slot_index[:, :, None] == jnp.arange(window_blocks)[None, None, :]).astype(jnp.float32)
    hd = jnp.einsum("asp,asij->aipj", onehot, hblocks, precision=HI)
    return hd.reshape(local_blocks * B, window_blocks * B)


def apply_ham(field, hdense):
    rows = field.shape[0]
    count = lax.axis_size("wide")
    swap_pairs = [(i, i ^ 1) for i in range(count)]
    cross_pairs = [(i, (i - 1) % count if i % 2 == 0 else (i + 1) % count) for i in range(count)]
    near_pairs = [(i, (i + 2) % count if (i // 2) % 2 == 0 else (i - 2) % count) for i in range(count)]
    wrap_pairs = [(i, (i - 2) % count if (i // 2) % 2 == 0 else (i + 2) % count) for i in range(count)]
    pieces = [
        lax.ppermute(field, "wide", near_pairs),
        lax.ppermute(field, "wide", swap_pairs),
        field,
        lax.ppermute(field, "wide", cross_pairs),
        lax.ppermute(field, "wide", wrap_pairs),
    ]
    total = None
    for idx in (2, 1, 3, 0, 4):
        term = jnp.dot(hdense[:, idx * rows:(idx + 1) * rows], pieces[idx], precision=HI,
                       preferred_element_type=jnp.float32)
        total = term if total is None else total + term
    return total


def local(subspace, hblocks, pattern, rotation):
    devcount = lax.axis_size("wide")
    myself = lax.axis_index("wide")
    owner = pattern // A_DEV
    relative = (owner - myself + HW + devcount) % devcount
    relative = jnp.where(myself % 2 == 0, jnp.where(relative == 1, 3, jnp.where(relative == 3, 1, relative)), relative)
    relative = jnp.where((myself // 2) % 2 == 0, jnp.where(relative == 0, 4, jnp.where(relative == 4, 0, relative)), relative)
    slot_index = relative * A_DEV + pattern % A_DEV
    hdense = dense_hamiltonian(hblocks, slot_index)
    subspace, probe_h = lax.optimization_barrier((subspace, hdense[:8, :128]))
    previous = subspace
    current = (apply_ham(subspace, hdense) - cheb_center * subspace) / cheb_half
    for step in range(DEGREE - 1):
        nextone = (
            2.0 * (apply_ham(current, hdense) - cheb_center * current) / cheb_half
            - previous
        )
        previous = current
        current = nextone
    total_rows = current.shape[0] * devcount
    gram_term = lax.dot_general(
        current,
        current,
        (((0,), (0,)), ((), ())),
        precision=HI,
        preferred_element_type=jnp.float32,
    )
    pieces = gram_term.reshape(devcount, -1, gram_term.shape[1])
    gathered = lax.all_to_all(pieces, "wide", 0, 0, tiled=True)
    correlation = jnp.sum(gathered, axis=0) / total_rows + 0.0 * probe_h[0, 0]
    rot_term = jnp.dot(
        current, rotation, precision=lax.Precision.HIGH, preferred_element_type=jnp.float32
    )
    rotated = lax.psum_scatter(rot_term, "grp", scatter_dimension=1, tiled=True)
    return (rotated, correlation)


def solution(mesh):
    in_specs = (P("wide", "grp"), P("wide", None, None, None), P("wide", None), P("grp", None))
    out_specs = (P("wide", "grp"), P(("grp", "wide"), None))
    return jax.shard_map(local, mesh=mesh, in_specs=in_specs, out_specs=out_specs, check_vma=False)
```
